32 devices in a mesh: group: 2 (over x), ctx: 16 (over z, y, core).
Axes of the slice: x: 2, y: 2, z: 4, core: 2. Of those that a mesh axis runs over, the one named last changes fastest.
Arguments:
- tokens: bfloat16 [16384, 1024], P(('group', 'ctx')), parts along dimension 0, may hold values from -140 to 140
- frames: int32 [16384], P(('group', 'ctx')), parts along dimension 0, may hold values from 0 to 31, never falling along the last dimension, each value on 1 to 1024 neighbouring positions
- norm_first: float32 [1024], replicated, may hold values from 0.5 to 1.5
- lin_query: bfloat16 [1024, 1024], replicated, may hold values from -0.1875 to 0.1875
- lin_key: bfloat16 [1024, 1024], replicated, may hold values from -0.1875 to 0.1875
- lin_value: bfloat16 [1024, 1024], replicated, may hold values from -0.1875 to 0.1875
- norm_mixed: float32 [1024], replicated, may hold values from 0.5 to 1.5
- lin_out: bfloat16 [1024, 1024], replicated, may hold values from -0.1875 to 0.1875
- norm_second: float32 [1024], replicated, may hold values from 0.5 to 1.5
- soft_query: bfloat16 [1024, 1024], replicated, may hold values from -8 to 8
- soft_key: bfloat16 [1024, 256], replicated, may hold values from -0.25 to 0.25
- soft_value: bfloat16 [1024, 256], replicated, may hold values from -0.1875 to 0.1875
Outputs:
- attended: bfloat16 [16384, 1024], P(('group', 'ctx')), parts along dimension 0
The draws below stay inside these ranges and needn't reach their ends.
There are 2 independent parts, one for each index of `group`. The reference program is written for one: setup_inputs(seed, part) draws one part's arguments, and reference() takes and returns one part's arrays. A program takes and returns all parts, laid end to end along the dimension named above; an argument that names none is the same for every part. Nothing has to cross between parts.
Inputs may be any that keep to these rules, and one draw needn't show every extreme that they name: Each of the 32 frames holds 1 to 1024 consecutive tokens and one holds exactly 1024; frame numbers never fall along the clip.
All inputs are finite; a program needn't handle non-finite values.
Results may differ from the reference program's by a relative error of at most 0.008.
Values may be sent and summed in bfloat16 or wider, within the bound.
A program may use at most 192 MiB of HBM per device.

```python
import math
import jax
import jax.numpy as jnp
import numpy as np
from jax import lax

H = 8
DK = 128
KVH = 2
SPAN = 256
TOK_DEV = 512
D = 1024
SEQ = 8192
FRAMES = 32
FRAME_MOST = 1024


def draw_tokens(key, part):
    base = jax.random.normal(jax.random.fold_in(key, 1), (SEQ, D), jnp.float32)
    return jnp.clip(base, -6.0, 6.0).astype(jnp.bfloat16)


def drawn_pair(key):
    limit = min(6.0 / math.sqrt(D), 0.1875)
    key_part = jax.random.normal(jax.random.fold_in(key, 21), (D, KVH * DK), jnp.float32) / math.sqrt(D)
    key_part = jnp.clip(key_part, -limit, limit)
    query_part = jax.random.normal(jax.random.fold_in(key, 24), (D, H * DK), jnp.float32) / math.sqrt(D)
    query_part = jnp.clip(query_part, -limit, limit)
    return (query_part, key_part)


def draw_soft_query(key, part):
    return drawn_pair(key)[0].astype(jnp.bfloat16)


def draw_soft_key(key, part):
    return drawn_pair(key)[1].astype(jnp.bfloat16)


def split_up(number_of, total, bound, skew):
    portions = [(1 << 20) // math.isqrt(rank ** skew) + 1 for rank in range(2, number_of + 1)]
    spare, counts = total - bound - (number_of - 1), [1] * (number_of - 1)
    while spare > 0:
        candidates = [i for i in range(number_of - 1) if counts[i] < bound]
        pool, budget = sum([portions[i] for i in candidates]), spare
        for i in candidates:
            more = min(bound - counts[i], max(1, budget * portions[i] // pool), spare)
            counts[i] = counts[i] + more
            spare = spare - more
    return np.array([bound] + counts)


def ragged(rng, count, total, most, lean):
    if count == 2:
        one = jax.random.randint(rng, (), max(1, total - most), min(most, total - 1) + 1)
        return jnp.stack([one, total - one])
    lengths = jnp.asarray(split_up(count, total, most, lean), jnp.int32)
    pairs = (count - 1) // 2
    giver, receiver = lengths[1:1 + 2 * pairs:2], lengths[2:2 + 2 * pairs:2]
    slack = jnp.minimum(giver - 1, most - receiver)
    passed = jax.random.randint(jax.random.fold_in(rng, 1), (pairs,), 0, 1 << 20) % (slack + 1)
    lengths = lengths.at[1:1 + 2 * pairs:2].set(giver - passed).at[2:2 + 2 * pairs:2].set(receiver + passed)
    return lengths[jax.random.permutation(jax.random.fold_in(rng, 2), count)]


def normal_values(key, dims, width, bound, held_as=jnp.bfloat16):
    array = jax.random.normal(key, dims, jnp.float32) * width
    return jnp.minimum(jnp.maximum(array, -bound), bound).astype(held_as)


def setup_inputs(seed: int = 0, part: int = 0) -> dict:
    streams_of = jax.random.split(jax.random.key(seed), 13)
    own_keys = jax.random.split(jax.random.fold_in(streams_of[12], part), 13)
    tokens = draw_tokens(jax.random.fold_in(jax.random.fold_in(streams_of[12], part), 71), part)
    frames = jnp.searchsorted(jnp.cumsum(ragged(own_keys[1], FRAMES, SEQ, FRAME_MOST, 1)), jnp.arange(SEQ), side="right").astype(jnp.int32)
    norm_first = jnp.clip(jax.random.uniform(streams_of[2], (D,), jnp.float32, 0.5, 1.5), 0.5, 1.5)
    lin_query = normal_values(streams_of[3], (D, D), D ** -0.5, 0.1875)
    lin_key = normal_values(streams_of[4], (D, D), D ** -0.5, 0.1875)
    lin_value = normal_values(streams_of[5], (D, D), D ** -0.5, 0.1875)
    norm_mixed = jnp.clip(jax.random.uniform(streams_of[6], (D,), jnp.float32, 0.5, 1.5), 0.5, 1.5)
    lin_out = normal_values(streams_of[7], (D, D), D ** -0.5, 0.1875)
    norm_second = jnp.clip(jax.random.uniform(streams_of[8], (D,), jnp.float32, 0.5, 1.5), 0.5, 1.5)
    soft_query = draw_soft_query(jax.random.fold_in(streams_of[12], 71), part)
    soft_key = draw_soft_key(jax.random.fold_in(streams_of[12], 71), part)
    soft_value = normal_values(streams_of[11], (D, KVH * DK), D ** -0.5, 0.1875)
    return dict(tokens=tokens, frames=frames, norm_first=norm_first, lin_query=lin_query, lin_key=lin_key, lin_value=lin_value, norm_mixed=norm_mixed, lin_out=lin_out, norm_second=norm_second, soft_query=soft_query, soft_key=soft_key, soft_value=soft_value)


epsilon = 1e-05

def rms_scaled(inputs, scales):
    inputs = inputs.astype(jnp.float32)
    mean_square = lax.optimization_barrier(jnp.mean(inputs * inputs, axis=-1, keepdims=True))
    return inputs * lax.rsqrt(mean_square + epsilon) * scales.astype(jnp.float32)

def project(inputs, weights):
    return jnp.dot(inputs, weights, preferred_element_type=jnp.float32)

def reference(tokens, frames, norm_first, lin_query, lin_key, lin_value, norm_mixed, lin_out, norm_second, soft_query, soft_key, soft_value):
    seq_len = tokens.shape[0]
    normed = rms_scaled(tokens, norm_first).astype(jnp.bfloat16)
    lin_q = jax.nn.silu(project(normed, lin_query)).astype(jnp.bfloat16)
    lin_k = jax.nn.silu(project(normed, lin_key)).astype(jnp.bfloat16)
    lin_v = project(normed, lin_value).astype(jnp.bfloat16)
    span_count = seq_len // SPAN
    span_q = lin_q.reshape(span_count, SPAN, H, DK).astype(jnp.float32)
    span_k = lin_k.reshape(span_count, SPAN, H, DK).astype(jnp.float32)
    span_v = lin_v.reshape(span_count, SPAN, H, DK).astype(jnp.float32)
    span_states = jnp.einsum('csha,cshb->chab', span_k, span_v)
    running = jnp.cumsum(span_states, axis=0)
    before = jnp.concatenate([jnp.zeros_like(running[:1]), running[:-1]], axis=0)
    inner = jnp.einsum('csha,ctha->chst', span_q, span_k)
    causal = jnp.arange(SPAN)[:, None] >= jnp.arange(SPAN)[None, :]
    inner = jnp.where(causal, inner, 0.0).astype(jnp.bfloat16)
    inner = lax.optimization_barrier(inner).astype(jnp.float32)
    local_part = jnp.einsum('chst,cthb->cshb', inner, span_v)
    carried = jnp.einsum('csha,chab->cshb', span_q, before, precision=lax.Precision.HIGHEST)
    mixed = (local_part + carried).reshape(seq_len, H * DK)
    lin_normed = rms_scaled(mixed, norm_mixed).astype(jnp.bfloat16)
    residual = tokens.astype(jnp.float32) + project(lin_normed, lin_out)
    normed_two = rms_scaled(residual, norm_second).astype(jnp.bfloat16)
    block_count = seq_len // TOK_DEV
    group_size = H // KVH
    soft_q = project(normed_two, soft_query).astype(jnp.bfloat16).reshape(block_count, TOK_DEV, KVH, group_size, DK)
    soft_k = project(normed_two, soft_key).astype(jnp.bfloat16).reshape(block_count, TOK_DEV, KVH, DK)
    soft_v = project(normed_two, soft_value).astype(jnp.bfloat16).reshape(block_count, TOK_DEV, KVH, DK)
    prior_k = jnp.concatenate([jnp.zeros_like(soft_k[:1]), soft_k[:-1]], axis=0)
    prior_v = jnp.concatenate([jnp.zeros_like(soft_v[:1]), soft_v[:-1]], axis=0)
    frame_blocks = frames.reshape(block_count, TOK_DEV)
    block_ids = jnp.arange(block_count, dtype=jnp.int32)
    scale = DK ** (-0.5)

    def attend_block(operands):
        block_q, own_k, own_v, last_k, last_v, frame_row, block_id = operands
        key_set = jnp.concatenate([last_k, own_k], axis=0).astype(jnp.float32)
        value_set = jnp.concatenate([last_v, own_v], axis=0).astype(jnp.float32)
        scores = jnp.einsum('qgrd,kgd->grqk', block_q.astype(jnp.float32), key_set) * scale
        own_mask = frame_row[None, :] <= frame_row[:, None]
        last_mask = jnp.broadcast_to(block_id > 0, (TOK_DEV, TOK_DEV))
        allowed = jnp.concatenate([last_mask, own_mask], axis=1)
        scores = jnp.where(allowed, scores, -1e+30)
        highest = lax.optimization_barrier(jnp.max(scores, axis=-1, keepdims=True))
        weights = jnp.exp(scores - highest)
        totals = lax.optimization_barrier(jnp.sum(weights, axis=-1, keepdims=True))
        probs = (weights / totals).astype(jnp.bfloat16)
        probs = lax.optimization_barrier(probs).astype(jnp.float32)
        return jnp.einsum('grqk,kgd->qgrd', probs, value_set).astype(jnp.bfloat16)
    attended = lax.map(attend_block, (soft_q, soft_k, soft_v, prior_k, prior_v, frame_blocks, block_ids))
    return attended.reshape(seq_len, H * DK)
```

```python
import functools
import math

import jax
import jax.numpy as jnp
from jax import lax
from jax.experimental import pallas as pl
from jax.experimental.pallas import tpu as pltpu
from jax.sharding import PartitionSpec as P

H = 8
DK = 128
KVH = 2
SPAN = 256
LANES = 4
PAIR = 2 * DK
epsilon = 1e-05
EXP2_SCALE = DK ** (-0.5) * math.log2(math.e)
F32 = jnp.float32
BF16 = jnp.bfloat16


def dot(a, b):
    return jnp.dot(a, b, preferred_element_type=F32)


def dot_t(a, b):
    return lax.dot_general(a, b, (((1,), (1,)), ((), ())), preferred_element_type=F32)


def t_dot(a, b):
    return lax.dot_general(a, b, (((0,), (0,)), ((), ())), preferred_element_type=F32)


def rms(x, gain):
    mean_square = jnp.mean(x * x, axis=-1, keepdims=True)
    return x * lax.rsqrt(mean_square + epsilon) * gain


def silu(v):
    return v / (1.0 + jnp.exp(-v))


def remote(src, dst, send_sem, recv_sem, ctx):
    return pltpu.make_async_remote_copy(
        src_ref=src,
        dst_ref=dst,
        send_sem=send_sem,
        recv_sem=recv_sem,
        device_id={"ctx": ctx},
        device_id_type=pl.DeviceIdType.MESH,
    )


def kernel(
    n,
    tok_hbm, frames_ref, g1_ref, gm_ref, g2_ref,
    wq_hbm, wk_hbm, wv_hbm, wo_hbm, sq_hbm, sk_hbm, sv_hbm,
    out_hbm,
    tok, wq, wk, wv, wo, sq, sk, sv,
    normed, lin_q, lin_k, lin_v, mixed, first_state,
    send_a, recv_a, send_b, recv_b, send_c, recv_c, earlier,
    soft_q, soft_kv, prior_kv, peak, acc, out_buf,
    load_sem, sa, ra, sb, rb, sc, rc, skv, rkv, out_sem,
):
    rows = tok.shape[0]
    groups = n // LANES
    ctx = lax.axis_index("ctx")
    me = lax.rem(ctx, LANES)
    group = lax.div(ctx, LANES)
    base = group * LANES

    loads = [
        pltpu.make_async_copy(src, dst, load_sem.at[i])
        for i, (src, dst) in enumerate(
            [(tok_hbm, tok), (wk_hbm, wk), (wv_hbm, wv), (wq_hbm, wq),
             (wo_hbm, wo), (sk_hbm, sk), (sv_hbm, sv), (sq_hbm, sq)]
        )
    ]
    for load in loads:
        load.start()

    barrier = pltpu.get_barrier_semaphore()

    def greet(who):
        pl.semaphore_signal(
            barrier, inc=1, device_id={"ctx": who}, device_id_type=pl.DeviceIdType.MESH
        )

    for i in range(1, LANES):
        greet(base + lax.rem(me + i, LANES))
    for i in range(1, groups):
        greet(lax.rem(group + i, groups) * LANES + me)

    @pl.when(me == 0)
    def _():
        greet(lax.rem(ctx + n - 1, n))

    @pl.when(me == LANES - 1)
    def _():
        greet(lax.rem(ctx + 1, n))

    loads[0].wait()
    for r in range(0, rows, 128):
        x = tok[r:r + 128, :].astype(F32)
        normed[r:r + 128, :] = rms(x, g1_ref[...]).astype(BF16)

    edge = jnp.where((me == 0) | (me == LANES - 1), 1, 0)
    pl.semaphore_wait(barrier, LANES - 1 + groups - 1 + edge)

    loads[1].wait()
    loads[2].wait()
    copies_a = []
    for i in range(LANES):
        pair = lax.rem(me + 1 + i, LANES)
        cols = pl.ds(pl.multiple_of(pair * PAIR, PAIR), PAIR)
        x = normed[...]
        k = silu(dot(x, wk[:, cols])).astype(BF16)
        v = dot(x, wv[:, cols]).astype(BF16)
        lin_k[:, cols] = k
        lin_v[:, cols] = v
        s0 = t_dot(k[:SPAN], v[:SPAN])
        s1 = t_dot(k[SPAN:], v[SPAN:])
        for j in range(2):
            d = slice(j * DK, (j + 1) * DK)
            first_state[pair, j] = s0[d, d]
            total = (s0[d, d] + s1[d, d]).astype(BF16)
            if i < LANES - 1:
                send_a[i, j] = total
            else:
                recv_a[me, j] = total
        if i < LANES - 1:
            copy = remote(send_a.at[i], recv_a.at[me], sa.at[i], ra.at[me], base + pair)
            copy.start()
            copies_a.append(copy)

    loads[3].wait()
    for p in range(LANES):
        cols = slice(p * PAIR, (p + 1) * PAIR)
        lin_q[:, cols] = silu(dot(normed[...], wq[:, cols])).astype(BF16)

    for i in range(1, LANES):
        src = lax.rem(me + i, LANES)
        remote(recv_a.at[src], recv_a.at[src], sa.at[0], ra.at[src], base + src).wait_recv()
    whole = recv_a[0].astype(F32)
    for j in range(1, LANES):
        whole = whole + recv_a[j].astype(F32)
    send_b[...] = whole.astype(BF16)

    def to_group(d, go):
        copy = remote(
            send_b, recv_b.at[group], sb.at[d], rb.at[group],
            lax.rem(ctx + (d + 1) * LANES, n),
        )

        @pl.when(group + d + 1 < groups)
        def _():
            if go:
                copy.start()
            else:
                copy.wait_send()

    for d in range(groups - 1):
        to_group(d, True)

    row = lax.broadcasted_iota(jnp.int32, (SPAN, SPAN), 0)
    col = lax.broadcasted_iota(jnp.int32, (SPAN, SPAN), 1)
    causal = row >= col
    for h in range(H):
        cols = slice(h * DK, (h + 1) * DK)
        for c in range(rows // SPAN):
            span = slice(c * SPAN, (c + 1) * SPAN)
            v = lin_v[span, cols]
            inner = dot_t(lin_q[span, cols], lin_k[span, cols])
            inner = jnp.where(causal, inner, 0.0).astype(BF16)
            mixed[span, cols] = dot(inner, v)

    earlier[...] = jnp.zeros_like(earlier)

    @pl.loop(0, group)
    def _(g):
        remote(recv_b.at[g], recv_b.at[g], sb.at[0], rb.at[g], base + lax.rem(me + 1, LANES)).wait_recv()
        earlier[...] += recv_b[g].astype(F32)

    prefix = earlier[...]
    for j in range(LANES):
        send_c[j] = prefix.astype(BF16)
        if j < LANES - 1:
            prefix = prefix + recv_a[j].astype(F32)
    copies_c = []
    for i in range(1, LANES):
        dst = lax.rem(me + i, LANES)
        copy = remote(send_c.at[dst], recv_c.at[me], sc.at[i - 1], rc.at[me], base + dst)
        copy.start()
        copies_c.append(copy)
    recv_c[me] = send_c[me]
    for i in range(1, LANES):
        src = lax.rem(me + i, LANES)
        remote(recv_c.at[src], recv_c.at[src], sc.at[0], rc.at[src], base + src).wait_recv()

    for h in range(H):
        cols = slice(h * DK, (h + 1) * DK)
        before = recv_c[h // 2, h % 2]
        mixed[:SPAN, cols] += dot(lin_q[:SPAN, cols], before)
        later = before.astype(F32) + first_state[h // 2, h % 2]
        high = later.astype(BF16)
        low = (later - high.astype(F32)).astype(BF16)
        q = lin_q[SPAN:, cols]
        mixed[SPAN:, cols] += dot(q, high) + dot(q, low)

    for r in range(0, rows, 128):
        normed[r:r + 128, :] = rms(mixed[r:r + 128, :], gm_ref[...]).astype(BF16)
    loads[4].wait()
    for p in range(LANES):
        cols = slice(p * PAIR, (p + 1) * PAIR)
        mixed[:, cols] = tok[:, cols].astype(F32) + dot(normed[...], wo[:, cols])
    for r in range(0, rows, 128):
        normed[r:r + 128, :] = rms(mixed[r:r + 128, :], g2_ref[...]).astype(BF16)

    loads[5].wait()
    loads[6].wait()
    soft_kv[0] = dot(normed[...], sk[...]).astype(BF16)
    soft_kv[1] = dot(normed[...], sv[...]).astype(BF16)
    following = lax.rem(ctx + 1, n)
    copy_kv = [
        remote(soft_kv.at[i], prior_kv.at[i], skv.at[i], rkv.at[i], following) for i in range(2)
    ]

    @pl.when(ctx < n - 1)
    def _():
        for copy in copy_kv:
            copy.start()

    loads[7].wait()
    for p in range(LANES):
        cols = slice(p * PAIR, (p + 1) * PAIR)
        soft_q[:, cols] = dot(normed[...], sq[:, cols]).astype(BF16)

    frames = frames_ref[...]
    ones = jnp.ones((rows, DK), BF16)
    half = rows // 2
    for r in range(0, rows, half):
        span = slice(r, r + half)
        mine = jnp.transpose(jnp.broadcast_to(frames[:, span], (DK, half)))[:, :1]
        allowed = frames <= mine
        for h in range(H):
            cols = slice(h * DK, (h + 1) * DK)
            kv = slice((h // (H // KVH)) * DK, (h // (H // KVH) + 1) * DK)
            s = dot_t(soft_q[span, cols], soft_kv[0, :, kv])
            s = jnp.where(allowed, s, -1e30)
            m = jnp.max(s, axis=-1, keepdims=True)
            w = jnp.exp2((s - m) * EXP2_SCALE).astype(BF16)
            acc[h, span, :] = dot(w, jnp.concatenate([soft_kv[1, :, kv], ones], axis=1))
            peak[h, span, :] = m

    @pl.when(ctx > 0)
    def _():
        for copy in copy_kv:
            copy.wait_recv()
        for h in range(H):
            for r in range(0, rows, half):
                span = slice(r, r + half)
                cols = slice(h * DK, (h + 1) * DK)
                kv = slice((h // (H // KVH)) * DK, (h // (H // KVH) + 1) * DK)
                s = dot_t(soft_q[span, cols], prior_kv[0, :, kv])
                before_m = peak[h, span, :]
                m = jnp.maximum(before_m, jnp.max(s, axis=-1, keepdims=True))
                w = jnp.exp2((s - m) * EXP2_SCALE).astype(BF16)
                scale = jnp.exp2((before_m - m) * EXP2_SCALE)
                both = acc[h, span, :] * scale + dot(
                    w, jnp.concatenate([prior_kv[1, :, kv], ones], axis=1)
                )
                out_buf[span, cols] = (both[:, :DK] / both[:, DK:]).astype(BF16)
            pltpu.make_async_copy(out_buf.at[:, cols], out_hbm.at[:, cols], out_sem.at[h]).start()

    @pl.when(ctx == 0)
    def _():
        for h in range(H):
            cols = slice(h * DK, (h + 1) * DK)
            both = acc[h]
            out_buf[:, cols] = (both[:, :DK] / both[:, DK:]).astype(BF16)
            pltpu.make_async_copy(out_buf.at[:, cols], out_hbm.at[:, cols], out_sem.at[h]).start()

    for copy in copies_a + copies_c:
        copy.wait_send()
    for d in range(groups - 1):
        to_group(d, False)

    @pl.when(ctx < n - 1)
    def _():
        for copy in copy_kv:
            copy.wait_send()

    for h in range(H):
        cols = slice(h * DK, (h + 1) * DK)
        pltpu.make_async_copy(out_buf.at[:, cols], out_hbm.at[:, cols], out_sem.at[h]).wait()


def body(
    n,
    tokens, frames, norm_first, lin_query, lin_key, lin_value, norm_mixed, lin_out,
    norm_second, soft_query, soft_key, soft_value,
):
    rows, width = tokens.shape
    groups = n // LANES
    any_spec = pl.BlockSpec(memory_space=pl.ANY)
    vmem = pl.BlockSpec(memory_space=pltpu.VMEM)
    dma = pltpu.SemaphoreType.DMA
    state = (2, DK, DK)
    return pl.pallas_call(
        functools.partial(kernel, n),
        out_shape=jax.ShapeDtypeStruct((rows, H * DK), BF16),
        in_specs=[any_spec, vmem, vmem, vmem, vmem] + [any_spec] * 7,
        out_specs=any_spec,
        scratch_shapes=[
            pltpu.VMEM((rows, width), BF16),
            pltpu.VMEM(lin_query.shape, BF16),
            pltpu.VMEM(lin_key.shape, BF16),
            pltpu.VMEM(lin_value.shape, BF16),
            pltpu.VMEM(lin_out.shape, BF16),
            pltpu.VMEM(soft_query.shape, BF16),
            pltpu.VMEM(soft_key.shape, BF16),
            pltpu.VMEM(soft_value.shape, BF16),
            pltpu.VMEM((rows, width), BF16),
            pltpu.VMEM((rows, H * DK), BF16),
            pltpu.VMEM((rows, H * DK), BF16),
            pltpu.VMEM((rows, H * DK), BF16),
            pltpu.VMEM((rows, H * DK), F32),
            pltpu.VMEM((LANES,) + state, F32),
            pltpu.VMEM((LANES - 1,) + state, BF16),
            pltpu.VMEM((LANES,) + state, BF16),
            pltpu.VMEM(state, BF16),
            pltpu.VMEM((groups,) + state, BF16),
            pltpu.VMEM((LANES,) + state, BF16),
            pltpu.VMEM((LANES,) + state, BF16),
            pltpu.VMEM(state, F32),
            pltpu.VMEM((rows, H * DK), BF16),
            pltpu.VMEM((2, rows, KVH * DK), BF16),
            pltpu.VMEM((2, rows, KVH * DK), BF16),
            pltpu.VMEM((H, rows, 1), F32),
            pltpu.VMEM((H, rows, 2 * DK), F32),
            pltpu.VMEM((rows, H * DK), BF16),
            dma((8,)),
            dma((LANES - 1,)),
            dma((LANES,)),
            dma((groups,)),
            dma((groups,)),
            dma((LANES - 1,)),
            dma((LANES,)),
            dma((2,)),
            dma((2,)),
            dma((H,)),
        ],
        compiler_params=pltpu.CompilerParams(
            collective_id=0, has_side_effects=True, vmem_limit_bytes=56 * 2**20
        ),
    )(
        tokens,
        frames.reshape(1, rows),
        norm_first.reshape(1, width),
        norm_mixed.reshape(1, H * DK),
        norm_second.reshape(1, width),
        lin_query, lin_key, lin_value, lin_out, soft_query, soft_key, soft_value,
    )


def solution(mesh):
    n = mesh.shape["ctx"]
    return jax.shard_map(
        functools.partial(body, n),
        mesh=mesh,
        in_specs=(P(("group", "ctx"), None), P(("group", "ctx"))) + (P(),) * 10,
        out_specs=P(("group", "ctx"), None),
        check_vma=False,
    )
```

```python
import functools
import math

import jax
import jax.numpy as jnp
from jax import lax
from jax.experimental import pallas as pl
from jax.experimental.pallas import tpu as pltpu
from jax.sharding import PartitionSpec as P

H = 8
DK = 128
KVH = 2
SPAN = 256
LANES = 4
CHUNKS = H // LANES
PART = LANES * DK
PAIR = 2 * DK
epsilon = 1e-05
EXP2_SCALE = DK ** (-0.5) * math.log2(math.e)
F32 = jnp.float32
BF16 = jnp.bfloat16


def dot(a, b):
    return jnp.dot(a, b, preferred_element_type=F32)


def dot_t(a, b):
    return lax.dot_general(a, b, (((1,), (1,)), ((), ())), preferred_element_type=F32)


def t_dot(a, b):
    return lax.dot_general(a, b, (((0,), (0,)), ((), ())), preferred_element_type=F32)


def rms(x, gain):
    mean_square = jnp.mean(x * x, axis=-1, keepdims=True)
    return x * lax.rsqrt(mean_square + epsilon) * gain


def silu(v):
    return v / (1.0 + jnp.exp(-v))


def remote(src, dst, send_sem, recv_sem, ctx):
    return pltpu.make_async_remote_copy(
        src_ref=src,
        dst_ref=dst,
        send_sem=send_sem,
        recv_sem=recv_sem,
        device_id={"ctx": ctx},
        device_id_type=pl.DeviceIdType.MESH,
    )


def kernel(
    n,
    tok_hbm, frames_ref, g1_ref, gm_ref, g2_ref,
    wq_hbm, wk_hbm, wv_hbm, wo_hbm, sq_hbm, sk_hbm, sv_hbm,
    out_hbm,
    tok, wq, wk, wv, wo, sq, sk, sv,
    normed, lin_q, lin_k, lin_v, mixed, first_state,
    send_a, recv_a, send_b, recv_b, send_c, recv_c, earlier,
    soft_q, soft_kv, prior_kv, peak, acc, out_buf,
    load_sem, sa, ra, sb, rb, sc, rc, skv, rkv, out_sem,
):
    rows = tok.shape[0]
    groups = n // LANES
    ctx = lax.axis_index("ctx")
    me = lax.rem(ctx, LANES)
    group = lax.div(ctx, LANES)
    base = group * LANES

    def load(i, src, dst):
        return pltpu.make_async_copy(src, dst, load_sem.at[i])

    def part(ref, c):
        return ref.at[:, c * PART:(c + 1) * PART]

    load_tok = load(0, tok_hbm, tok)
    load_kv = [
        [load(1 + 2 * c, part(wk_hbm, c), part(wk, c)), load(2 + 2 * c, part(wv_hbm, c), part(wv, c))]
        for c in range(CHUNKS)
    ]
    load_q = load(1 + 2 * CHUNKS, wq_hbm, wq)
    load_o = load(2 + 2 * CHUNKS, wo_hbm, wo)
    load_soft = [
        load(3 + 2 * CHUNKS + i, src, dst)
        for i, (src, dst) in enumerate([(sk_hbm, sk), (sv_hbm, sv), (sq_hbm, sq)])
    ]
    load_tok.start()
    for copy in load_kv[0]:
        copy.start()

    barrier = pltpu.get_barrier_semaphore()

    def greet(who):
        pl.semaphore_signal(
            barrier, inc=1, device_id={"ctx": who}, device_id_type=pl.DeviceIdType.MESH
        )

    for i in range(1, LANES):
        greet(base + lax.rem(me + i, LANES))
    for i in range(1, groups):
        greet(lax.rem(group + i, groups) * LANES + me)

    @pl.when(me == 0)
    def _():
        greet(lax.rem(ctx + n - 1, n))

    @pl.when(me == LANES - 1)
    def _():
        greet(lax.rem(ctx + 1, n))

    load_tok.wait()
    for c in range(1, CHUNKS):
        for copy in load_kv[c]:
            copy.start()
    for r in range(0, rows, 128):
        x = tok[r:r + 128, :].astype(F32)
        normed[r:r + 128, :] = rms(x, g1_ref[...]).astype(BF16)

    edge = jnp.where((me == 0) | (me == LANES - 1), 1, 0)
    pl.semaphore_wait(barrier, LANES - 1 + groups - 1 + edge)

    copies_a = []
    for c in range(CHUNKS):
        for copy in load_kv[c]:
            copy.wait()
        if c == 0:
            load_q.start()
            load_o.start()
        for p in range(c * LANES // 2, (c + 1) * LANES // 2):
            cols = slice(p * PAIR, (p + 1) * PAIR)
            x = normed[...]
            k = silu(dot(x, wk[:, cols])).astype(BF16)
            v = dot(x, wv[:, cols]).astype(BF16)
            lin_k[:, cols] = k
            lin_v[:, cols] = v
            s0 = t_dot(k[:SPAN], v[:SPAN])
            s1 = t_dot(k[SPAN:], v[SPAN:])
            for j in range(2):
                h = 2 * p + j
                d = slice(j * DK, (j + 1) * DK)
                first_state[h] = s0[d, d]
                send_a[c, h % LANES] = (s0[d, d] + s1[d, d]).astype(BF16)
        recv_a[c, me] = send_a[c, me]
        for i in range(1, LANES):
            dst = lax.rem(me + i, LANES)
            copy = remote(
                send_a.at[c, dst], recv_a.at[c, me], sa.at[c, i - 1], ra.at[c, me], base + dst
            )
            copy.start()
            copies_a.append(copy)
    for copy in load_soft:
        copy.start()

    def to_group(c, d, go):
        copy = remote(
            send_b.at[c], recv_b.at[c, group], sb.at[c, d], rb.at[c, group],
            lax.rem(ctx + (d + 1) * LANES, n),
        )

        @pl.when(group + d + 1 < groups)
        def _():
            if go:
                copy.start()
            else:
                copy.wait_send()

    def group_total(c):
        for i in range(1, LANES):
            src = lax.rem(me + i, LANES)
            remote(
                recv_a.at[c, src], recv_a.at[c, src], sa.at[c, 0], ra.at[c, src], base + src
            ).wait_recv()
        whole = recv_a[c, 0].astype(F32)
        for j in range(1, LANES):
            whole = whole + recv_a[c, j].astype(F32)
        send_b[c] = whole.astype(BF16)
        for d in range(groups - 1):
            to_group(c, d, True)

    load_q.wait()
    for c in range(CHUNKS):
        group_total(c)
        for p in range(c * LANES // 2, (c + 1) * LANES // 2):
            cols = slice(p * PAIR, (p + 1) * PAIR)
            lin_q[:, cols] = silu(dot(normed[...], wq[:, cols])).astype(BF16)

    row = lax.broadcasted_iota(jnp.int32, (SPAN, SPAN), 0)
    col = lax.broadcasted_iota(jnp.int32, (SPAN, SPAN), 1)
    causal = row >= col
    for h in range(H):
        cols = slice(h * DK, (h + 1) * DK)
        for c in range(rows // SPAN):
            span = slice(c * SPAN, (c + 1) * SPAN)
            v = lin_v[span, cols]
            inner = dot_t(lin_q[span, cols], lin_k[span, cols])
            inner = jnp.where(causal, inner, 0.0).astype(BF16)
            mixed[span, cols] = dot(inner, v)

    copies_c = []
    for c in range(CHUNKS):
        earlier[...] = jnp.zeros_like(earlier)

        @pl.loop(0, group)
        def _(g):
            remote(
                recv_b.at[c, g], recv_b.at[c, g], sb.at[c, 0], rb.at[c, g],
                base + lax.rem(me + 1, LANES),
            ).wait_recv()
            earlier[...] += recv_b[c, g].astype(F32)

        prefix = earlier[...]
        for j in range(LANES):
            send_c[c, j] = prefix.astype(BF16)
            if j < LANES - 1:
                prefix = prefix + recv_a[c, j].astype(F32)
        for i in range(1, LANES):
            dst = lax.rem(me + i, LANES)
            copy = remote(
                send_c.at[c, dst], recv_c.at[c, me], sc.at[c, i - 1], rc.at[c, me], base + dst
            )
            copy.start()
            copies_c.append(copy)
        recv_c[c, me] = send_c[c, me]

    for c in range(CHUNKS):
        for i in range(1, LANES):
            src = lax.rem(me + i, LANES)
            remote(
                recv_c.at[c, src], recv_c.at[c, src], sc.at[c, 0], rc.at[c, src], base + src
            ).wait_recv()
        for j in range(LANES):
            h = c * LANES + j
            cols = slice(h * DK, (h + 1) * DK)
            before = recv_c[c, j]
            mixed[:SPAN, cols] += dot(lin_q[:SPAN, cols], before)
            later = before.astype(F32) + first_state[h]
            high = later.astype(BF16)
            low = (later - high.astype(F32)).astype(BF16)
            q = lin_q[SPAN:, cols]
            mixed[SPAN:, cols] += dot(q, high) + dot(q, low)

    for r in range(0, rows, 128):
        normed[r:r + 128, :] = rms(mixed[r:r + 128, :], gm_ref[...]).astype(BF16)
    load_o.wait()
    for p in range(LANES):
        cols = slice(p * PAIR, (p + 1) * PAIR)
        mixed[:, cols] = tok[:, cols].astype(F32) + dot(normed[...], wo[:, cols])
    for r in range(0, rows, 128):
        normed[r:r + 128, :] = rms(mixed[r:r + 128, :], g2_ref[...]).astype(BF16)

    load_soft[0].wait()
    load_soft[1].wait()
    soft_kv[0] = dot(normed[...], sk[...]).astype(BF16)
    soft_kv[1] = dot(normed[...], sv[...]).astype(BF16)
    following = lax.rem(ctx + 1, n)
    copy_kv = [
        remote(soft_kv.at[i], prior_kv.at[i], skv.at[i], rkv.at[i], following) for i in range(2)
    ]

    @pl.when(ctx < n - 1)
    def _():
        for copy in copy_kv:
            copy.start()

    load_soft[2].wait()
    for p in range(LANES):
        cols = slice(p * PAIR, (p + 1) * PAIR)
        soft_q[:, cols] = dot(normed[...], sq[:, cols]).astype(BF16)

    frames = frames_ref[...]
    ones = jnp.ones((rows, DK), BF16)
    half = rows // 2
    for r in range(0, rows, half):
        span = slice(r, r + half)
        mine = jnp.transpose(jnp.broadcast_to(frames[:, span], (DK, half)))[:, :1]
        allowed = frames <= mine
        for h in range(H):
            cols = slice(h * DK, (h + 1) * DK)
            kv = slice((h // (H // KVH)) * DK, (h // (H // KVH) + 1) * DK)
            s = dot_t(soft_q[span, cols], soft_kv[0, :, kv])
            s = jnp.where(allowed, s, -1e30)
            m = jnp.max(s, axis=-1, keepdims=True)
            w = jnp.exp2((s - m) * EXP2_SCALE).astype(BF16)
            acc[h, span, :] = dot(w, jnp.concatenate([soft_kv[1, :, kv], ones], axis=1))
            peak[h, span, :] = m

    @pl.when(ctx > 0)
    def _():
        for copy in copy_kv:
            copy.wait_recv()
        for h in range(H):
            for r in range(0, rows, half):
                span = slice(r, r + half)
                cols = slice(h * DK, (h + 1) * DK)
                kv = slice((h // (H // KVH)) * DK, (h // (H // KVH) + 1) * DK)
                s = dot_t(soft_q[span, cols], prior_kv[0, :, kv])
                before_m = peak[h, span, :]
                m = jnp.maximum(before_m, jnp.max(s, axis=-1, keepdims=True))
                w = jnp.exp2((s - m) * EXP2_SCALE).astype(BF16)
                scale = jnp.exp2((before_m - m) * EXP2_SCALE)
                both = acc[h, span, :] * scale + dot(
                    w, jnp.concatenate([prior_kv[1, :, kv], ones], axis=1)
                )
                out_buf[span, cols] = (both[:, :DK] / both[:, DK:]).astype(BF16)
            pltpu.make_async_copy(out_buf.at[:, cols], out_hbm.at[:, cols], out_sem.at[h]).start()

    @pl.when(ctx == 0)
    def _():
        for h in range(H):
            cols = slice(h * DK, (h + 1) * DK)
            both = acc[h]
            out_buf[:, cols] = (both[:, :DK] / both[:, DK:]).astype(BF16)
            pltpu.make_async_copy(out_buf.at[:, cols], out_hbm.at[:, cols], out_sem.at[h]).start()

    for copy in copies_a + copies_c:
        copy.wait_send()
    for c in range(CHUNKS):
        for d in range(groups - 1):
            to_group(c, d, False)

    @pl.when(ctx < n - 1)
    def _():
        for copy in copy_kv:
            copy.wait_send()

    for h in range(H):
        cols = slice(h * DK, (h + 1) * DK)
        pltpu.make_async_copy(out_buf.at[:, cols], out_hbm.at[:, cols], out_sem.at[h]).wait()


def body(
    n,
    tokens, frames, norm_first, lin_query, lin_key, lin_value, norm_mixed, lin_out,
    norm_second, soft_query, soft_key, soft_value,
):
    rows, width = tokens.shape
    groups = n // LANES
    any_spec = pl.BlockSpec(memory_space=pl.ANY)
    vmem = pl.BlockSpec(memory_space=pltpu.VMEM)
    dma = pltpu.SemaphoreType.DMA
    state = (DK, DK)
    return pl.pallas_call(
        functools.partial(kernel, n),
        out_shape=jax.ShapeDtypeStruct((rows, H * DK), BF16),
        in_specs=[any_spec, vmem, vmem, vmem, vmem] + [any_spec] * 7,
        out_specs=any_spec,
        scratch_shapes=[
            pltpu.VMEM((rows, width), BF16),
            pltpu.VMEM(lin_query.shape, BF16),
            pltpu.VMEM(lin_key.shape, BF16),
            pltpu.VMEM(lin_value.shape, BF16),
            pltpu.VMEM(lin_out.shape, BF16),
            pltpu.VMEM(soft_query.shape, BF16),
            pltpu.VMEM(soft_key.shape, BF16),
            pltpu.VMEM(soft_value.shape, BF16),
            pltpu.VMEM((rows, width), BF16),
            pltpu.VMEM((rows, H * DK), BF16),
            pltpu.VMEM((rows, H * DK), BF16),
            pltpu.VMEM((rows, H * DK), BF16),
            pltpu.VMEM((rows, H * DK), F32),
            pltpu.VMEM((H,) + state, F32),
            pltpu.VMEM((CHUNKS, LANES) + state, BF16),
            pltpu.VMEM((CHUNKS, LANES) + state, BF16),
            pltpu.VMEM((CHUNKS,) + state, BF16),
            pltpu.VMEM((CHUNKS, groups) + state, BF16),
            pltpu.VMEM((CHUNKS, LANES) + state, BF16),
            pltpu.VMEM((CHUNKS, LANES) + state, BF16),
            pltpu.VMEM(state, F32),
            pltpu.VMEM((rows, H * DK), BF16),
            pltpu.VMEM((2, rows, KVH * DK), BF16),
            pltpu.VMEM((2, rows, KVH * DK), BF16),
            pltpu.VMEM((H, rows, 1), F32),
            pltpu.VMEM((H, rows, 2 * DK), F32),
            pltpu.VMEM((rows, H * DK), BF16),
            dma((6 + 2 * CHUNKS,)),
            dma((CHUNKS, LANES - 1)),
            dma((CHUNKS, LANES)),
            dma((CHUNKS, groups)),
            dma((CHUNKS, groups)),
            dma((CHUNKS, LANES - 1)),
            dma((CHUNKS, LANES)),
            dma((2,)),
            dma((2,)),
            dma((H,)),
        ],
        compiler_params=pltpu.CompilerParams(
            collective_id=0, has_side_effects=True, vmem_limit_bytes=56 * 2**20
        ),
    )(
        tokens,
        frames.reshape(1, rows),
        norm_first.reshape(1, width),
        norm_mixed.reshape(1, H * DK),
        norm_second.reshape(1, width),
        lin_query, lin_key, lin_value, lin_out, soft_query, soft_key, soft_value,
    )


def solution(mesh):
    n = mesh.shape["ctx"]
    return jax.shard_map(
        functools.partial(body, n),
        mesh=mesh,
        in_specs=(P(("group", "ctx"), None), P(("group", "ctx"))) + (P(),) * 10,
        out_specs=P(("group", "ctx"), None),
        check_vma=False,
    )
```

```python
import functools
import math

import jax
import jax.numpy as jnp
from jax import lax
from jax.experimental import pallas as pl
from jax.experimental.pallas import tpu as pltpu
from jax.sharding import PartitionSpec as P

H = 8
DK = 128
KVH = 2
SPAN = 256
LANES = 4
CHUNKS = H // LANES
PART = LANES * DK
PAIR = 2 * DK
epsilon = 1e-05
EXP2_SCALE = DK ** (-0.5) * math.log2(math.e)
F32 = jnp.float32
BF16 = jnp.bfloat16


def dot(a, b):
    return jnp.dot(a, b, preferred_element_type=F32)


def dot_t(a, b):
    return lax.dot_general(a, b, (((1,), (1,)), ((), ())), preferred_element_type=F32)


def t_dot(a, b):
    return lax.dot_general(a, b, (((0,), (0,)), ((), ())), preferred_element_type=F32)


def rms(x, gain):
    mean_square = jnp.mean(x * x, axis=-1, keepdims=True)
    return x * lax.rsqrt(mean_square + epsilon) * gain


def silu(v):
    return v / (1.0 + jnp.exp(-v))


def remote(src, dst, send_sem, recv_sem, ctx):
    return pltpu.make_async_remote_copy(
        src_ref=src,
        dst_ref=dst,
        send_sem=send_sem,
        recv_sem=recv_sem,
        device_id={"ctx": ctx},
        device_id_type=pl.DeviceIdType.MESH,
    )


def kernel(
    n,
    tok_hbm, frames_ref, g1_ref, gm_ref, g2_ref,
    wq_hbm, wk_hbm, wv_hbm, wo_hbm, sq_hbm, sk_hbm, sv_hbm,
    out_hbm,
    tok, wq, wk, wv, wo, sq, sk, sv,
    normed, lin_q, lin_k, lin_v, mixed, first_state,
    send_a, recv_a, send_b, recv_b, send_c, recv_c, earlier,
    soft_q, soft_kv, prior_kv, peak, acc, out_buf,
    load_sem, sa, ra, sb, rb, sc, rc, skv, rkv, out_sem,
):
    rows = tok.shape[0]
    groups = n // LANES
    ctx = lax.axis_index("ctx")
    me = lax.rem(ctx, LANES)
    group = lax.div(ctx, LANES)
    base = group * LANES

    def load(i, src, dst):
        return pltpu.make_async_copy(src, dst, load_sem.at[i])

    def part(ref, c):
        return ref.at[:, c * PART:(c + 1) * PART]

    load_tok = load(0, tok_hbm, tok)
    load_kv = [
        [load(1 + 2 * c, part(wk_hbm, c), part(wk, c)), load(2 + 2 * c, part(wv_hbm, c), part(wv, c))]
        for c in range(CHUNKS)
    ]
    load_q = load(1 + 2 * CHUNKS, wq_hbm, wq)
    load_o = load(2 + 2 * CHUNKS, wo_hbm, wo)
    load_soft = [
        load(3 + 2 * CHUNKS + i, src, dst)
        for i, (src, dst) in enumerate([(sk_hbm, sk), (sv_hbm, sv), (sq_hbm, sq)])
    ]
    load_tok.start()
    for copy in load_kv[0]:
        copy.start()

    barrier = pltpu.get_barrier_semaphore()

    def greet(who):
        pl.semaphore_signal(
            barrier, inc=1, device_id={"ctx": who}, device_id_type=pl.DeviceIdType.MESH
        )

    for i in range(1, LANES):
        greet(base + lax.rem(me + i, LANES))
    for i in range(1, groups):
        greet(lax.rem(group + i, groups) * LANES + me)

    @pl.when(me == 0)
    def _():
        greet(lax.rem(ctx + n - 1, n))

    @pl.when(me == LANES - 1)
    def _():
        greet(lax.rem(ctx + 1, n))

    load_tok.wait()
    for c in range(1, CHUNKS):
        for copy in load_kv[c]:
            copy.start()
    for r in range(0, rows, 128):
        x = tok[r:r + 128, :].astype(F32)
        normed[r:r + 128, :] = rms(x, g1_ref[...]).astype(BF16)

    copies_a = []
    for c in range(CHUNKS):
        for copy in load_kv[c]:
            copy.wait()
        if c == 0:
            load_q.start()
            load_o.start()
        for p in range(c * LANES // 2, (c + 1) * LANES // 2):
            cols = slice(p * PAIR, (p + 1) * PAIR)
            x = normed[...]
            k = silu(dot(x, wk[:, cols])).astype(BF16)
            v = dot(x, wv[:, cols]).astype(BF16)
            lin_k[:, cols] = k
            lin_v[:, cols] = v
            s0 = t_dot(k[:SPAN], v[:SPAN])
            s1 = t_dot(k[SPAN:], v[SPAN:])
            for j in range(2):
                h = 2 * p + j
                d = slice(j * DK, (j + 1) * DK)
                first_state[h] = s0[d, d]
                send_a[c, h % LANES] = (s0[d, d] + s1[d, d]).astype(BF16)
        if c == 0:
            edge = jnp.where((me == 0) | (me == LANES - 1), 1, 0)
            pl.semaphore_wait(barrier, LANES - 1 + groups - 1 + edge)
        recv_a[c, me] = send_a[c, me]
        for i in range(1, LANES):
            dst = lax.rem(me + i, LANES)
            copy = remote(
                send_a.at[c, dst], recv_a.at[c, me], sa.at[c, i - 1], ra.at[c, me], base + dst
            )
            copy.start()
            copies_a.append(copy)
    for copy in load_soft:
        copy.start()

    def to_group(c, d, go):
        copy = remote(
            send_b.at[c], recv_b.at[c, group], sb.at[c, d], rb.at[c, group],
            lax.rem(ctx + (d + 1) * LANES, n),
        )

        @pl.when(group + d + 1 < groups)
        def _():
            if go:
                copy.start()
            else:
                copy.wait_send()

    def group_total(c):
        for i in range(1, LANES):
            src = lax.rem(me + i, LANES)
            remote(
                recv_a.at[c, src], recv_a.at[c, src], sa.at[c, 0], ra.at[c, src], base + src
            ).wait_recv()
        whole = recv_a[c, 0].astype(F32)
        for j in range(1, LANES):
            whole = whole + recv_a[c, j].astype(F32)
        send_b[c] = whole.astype(BF16)
        for d in range(groups - 1):
            to_group(c, d, True)

    load_q.wait()
    for c in range(CHUNKS):
        group_total(c)
        for p in range(c * LANES // 2, (c + 1) * LANES // 2):
            cols = slice(p * PAIR, (p + 1) * PAIR)
            lin_q[:, cols] = silu(dot(normed[...], wq[:, cols])).astype(BF16)

    row = lax.broadcasted_iota(jnp.int32, (SPAN, SPAN), 0)
    col = lax.broadcasted_iota(jnp.int32, (SPAN, SPAN), 1)
    causal = row >= col
    for h in range(H):
        cols = slice(h * DK, (h + 1) * DK)
        for c in range(rows // SPAN):
            span = slice(c * SPAN, (c + 1) * SPAN)
            v = lin_v[span, cols]
            inner = dot_t(lin_q[span, cols], lin_k[span, cols])
            inner = jnp.where(causal, inner, 0.0).astype(BF16)
            mixed[span, cols] = dot(inner, v)

    copies_c = []
    for c in range(CHUNKS):
        earlier[...] = jnp.zeros_like(earlier)

        @pl.loop(0, group)
        def _(g):
            remote(
                recv_b.at[c, g], recv_b.at[c, g], sb.at[c, 0], rb.at[c, g],
                base + lax.rem(me + 1, LANES),
            ).wait_recv()
            earlier[...] += recv_b[c, g].astype(F32)

        prefix = earlier[...]
        for j in range(LANES):
            send_c[c, j] = prefix.astype(BF16)
            if j < LANES - 1:
                prefix = prefix + recv_a[c, j].astype(F32)
        for i in range(1, LANES):
            dst = lax.rem(me + i, LANES)
            copy = remote(
                send_c.at[c, dst], recv_c.at[c, me], sc.at[c, i - 1], rc.at[c, me], base + dst
            )
            copy.start()
            copies_c.append(copy)
        recv_c[c, me] = send_c[c, me]

    for c in range(CHUNKS):
        for i in range(1, LANES):
            src = lax.rem(me + i, LANES)
            remote(
                recv_c.at[c, src], recv_c.at[c, src], sc.at[c, 0], rc.at[c, src], base + src
            ).wait_recv()
        for j in range(LANES):
            h = c * LANES + j
            cols = slice(h * DK, (h + 1) * DK)
            before = recv_c[c, j]
            mixed[:SPAN, cols] += dot(lin_q[:SPAN, cols], before)
            later = before.astype(F32) + first_state[h]
            high = later.astype(BF16)
            low = (later - high.astype(F32)).astype(BF16)
            q = lin_q[SPAN:, cols]
            mixed[SPAN:, cols] += dot(q, high) + dot(q, low)

    for r in range(0, rows, 128):
        normed[r:r + 128, :] = rms(mixed[r:r + 128, :], gm_ref[...]).astype(BF16)
    load_o.wait()
    for p in range(LANES):
        cols = slice(p * PAIR, (p + 1) * PAIR)
        mixed[:, cols] = tok[:, cols].astype(F32) + dot(normed[...], wo[:, cols])
    for r in range(0, rows, 128):
        normed[r:r + 128, :] = rms(mixed[r:r + 128, :], g2_ref[...]).astype(BF16)

    load_soft[0].wait()
    load_soft[1].wait()
    soft_kv[0] = dot(normed[...], sk[...]).astype(BF16)
    soft_kv[1] = dot(normed[...], sv[...]).astype(BF16)
    following = lax.rem(ctx + 1, n)
    copy_kv = [
        remote(soft_kv.at[i], prior_kv.at[i], skv.at[i], rkv.at[i], following) for i in range(2)
    ]

    @pl.when(ctx < n - 1)
    def _():
        for copy in copy_kv:
            copy.start()

    load_soft[2].wait()
    for p in range(LANES):
        cols = slice(p * PAIR, (p + 1) * PAIR)
        soft_q[:, cols] = dot(normed[...], sq[:, cols]).astype(BF16)

    frames = frames_ref[...]
    ones = jnp.ones((rows, DK), BF16)
    half = rows // 2
    for r in range(0, rows, half):
        span = slice(r, r + half)
        mine = jnp.transpose(jnp.broadcast_to(frames[:, span], (DK, half)))[:, :1]
        allowed = frames <= mine
        for h in range(H):
            cols = slice(h * DK, (h + 1) * DK)
            kv = slice((h // (H // KVH)) * DK, (h // (H // KVH) + 1) * DK)
            s = dot_t(soft_q[span, cols], soft_kv[0, :, kv])
            s = jnp.where(allowed, s, -1e30)
            m = jnp.max(s, axis=-1, keepdims=True)
            w = jnp.exp2((s - m) * EXP2_SCALE).astype(BF16)
            acc[h, span, :] = dot(w, jnp.concatenate([soft_kv[1, :, kv], ones], axis=1))
            peak[h, span, :] = m

    @pl.when(ctx > 0)
    def _():
        for copy in copy_kv:
            copy.wait_recv()
        for h in range(H):
            for r in range(0, rows, half):
                span = slice(r, r + half)
                cols = slice(h * DK, (h + 1) * DK)
                kv = slice((h // (H // KVH)) * DK, (h // (H // KVH) + 1) * DK)
                s = dot_t(soft_q[span, cols], prior_kv[0, :, kv])
                before_m = peak[h, span, :]
                m = jnp.maximum(before_m, jnp.max(s, axis=-1, keepdims=True))
                w = jnp.exp2((s - m) * EXP2_SCALE).astype(BF16)
                scale = jnp.exp2((before_m - m) * EXP2_SCALE)
                both = acc[h, span, :] * scale + dot(
                    w, jnp.concatenate([prior_kv[1, :, kv], ones], axis=1)
                )
                out_buf[span, cols] = (both[:, :DK] / both[:, DK:]).astype(BF16)
            pltpu.make_async_copy(out_buf.at[:, cols], out_hbm.at[:, cols], out_sem.at[h]).start()

    @pl.when(ctx == 0)
    def _():
        for h in range(H):
            cols = slice(h * DK, (h + 1) * DK)
            both = acc[h]
            out_buf[:, cols] = (both[:, :DK] / both[:, DK:]).astype(BF16)
            pltpu.make_async_copy(out_buf.at[:, cols], out_hbm.at[:, cols], out_sem.at[h]).start()

    for copy in copies_a + copies_c:
        copy.wait_send()
    for c in range(CHUNKS):
        for d in range(groups - 1):
            to_group(c, d, False)

    @pl.when(ctx < n - 1)
    def _():
        for copy in copy_kv:
            copy.wait_send()

    for h in range(H):
        cols = slice(h * DK, (h + 1) * DK)
        pltpu.make_async_copy(out_buf.at[:, cols], out_hbm.at[:, cols], out_sem.at[h]).wait()


def body(
    n,
    tokens, frames, norm_first, lin_query, lin_key, lin_value, norm_mixed, lin_out,
    norm_second, soft_query, soft_key, soft_value,
):
    rows, width = tokens.shape
    groups = n // LANES
    any_spec = pl.BlockSpec(memory_space=pl.ANY)
    vmem = pl.BlockSpec(memory_space=pltpu.VMEM)
    dma = pltpu.SemaphoreType.DMA
    state = (DK, DK)
    return pl.pallas_call(
        functools.partial(kernel, n),
        out_shape=jax.ShapeDtypeStruct((rows, H * DK), BF16),
        in_specs=[any_spec, vmem, vmem, vmem, vmem] + [any_spec] * 7,
        out_specs=any_spec,
        scratch_shapes=[
            pltpu.VMEM((rows, width), BF16),
            pltpu.VMEM(lin_query.shape, BF16),
            pltpu.VMEM(lin_key.shape, BF16),
            pltpu.VMEM(lin_value.shape, BF16),
            pltpu.VMEM(lin_out.shape, BF16),
            pltpu.VMEM(soft_query.shape, BF16),
            pltpu.VMEM(soft_key.shape, BF16),
            pltpu.VMEM(soft_value.shape, BF16),
            pltpu.VMEM((rows, width), BF16),
            pltpu.VMEM((rows, H * DK), BF16),
            pltpu.VMEM((rows, H * DK), BF16),
            pltpu.VMEM((rows, H * DK), BF16),
            pltpu.VMEM((rows, H * DK), F32),
            pltpu.VMEM((H,) + state, F32),
            pltpu.VMEM((CHUNKS, LANES) + state, BF16),
            pltpu.VMEM((CHUNKS, LANES) + state, BF16),
            pltpu.VMEM((CHUNKS,) + state, BF16),
            pltpu.VMEM((CHUNKS, groups) + state, BF16),
            pltpu.VMEM((CHUNKS, LANES) + state, BF16),
            pltpu.VMEM((CHUNKS, LANES) + state, BF16),
            pltpu.VMEM(state, F32),
            pltpu.VMEM((rows, H * DK), BF16),
            pltpu.VMEM((2, rows, KVH * DK), BF16),
            pltpu.VMEM((2, rows, KVH * DK), BF16),
            pltpu.VMEM((H, rows, 1), F32),
            pltpu.VMEM((H, rows, 2 * DK), F32),
            pltpu.VMEM((rows, H * DK), BF16),
            dma((6 + 2 * CHUNKS,)),
            dma((CHUNKS, LANES - 1)),
            dma((CHUNKS, LANES)),
            dma((CHUNKS, groups)),
            dma((CHUNKS, groups)),
            dma((CHUNKS, LANES - 1)),
            dma((CHUNKS, LANES)),
            dma((2,)),
            dma((2,)),
            dma((H,)),
        ],
        compiler_params=pltpu.CompilerParams(
            collective_id=0, has_side_effects=True, vmem_limit_bytes=56 * 2**20
        ),
    )(
        tokens,
        frames.reshape(1, rows),
        norm_first.reshape(1, width),
        norm_mixed.reshape(1, H * DK),
        norm_second.reshape(1, width),
        lin_query, lin_key, lin_value, lin_out, soft_query, soft_key, soft_value,
    )


def solution(mesh):
    n = mesh.shape["ctx"]
    return jax.shard_map(
        functools.partial(body, n),
        mesh=mesh,
        in_specs=(P(("group", "ctx"), None), P(("group", "ctx"))) + (P(),) * 10,
        out_specs=P(("group", "ctx"), None),
        check_vma=False,
    )
```
